32 devices in a mesh: frame: 4 (over y, x), head: 8 (over z, core).
Axes of the slice: x: 2, y: 2, z: 4, core: 2. Of those that a mesh axis runs over, the one named last changes fastest.
Arguments:
- tokens: float32 [8, 1024, 1024], P('frame', 'head'), may hold values from -48 to 48
- qkv_weight: float32 [1024, 3072], replicated
- out_weight: float32 [1024, 1024], replicated, may hold values from -0.1875 to 0.1875
- norm_gain: float32 [1024], replicated, may hold values from 0.1 to 1.9
- proj_weight: float32 [1024, 256], replicated, may hold values from -0.1875 to 0.1875
- up_weight: bfloat16 [256, 4096], replicated, may hold values from -0.375 to 0.375
- conv_weight: bfloat16 [2, 3, 3, 256, 256], replicated, may hold values from -0.125 to 0.125
- conv_bias: float32 [2, 256], replicated, may hold values from -3 to 3
- block_lists: int32 [64, 13], P('frame'), may hold values from 0 to 63, as said below
- block_counts: int32 [64], P('frame'), may hold values from 1 to 13, as said below
Outputs:
- refined: bfloat16 [8, 128, 128, 256], P('frame', 'head')
The draws below stay inside these ranges and needn't reach their ends.
Inputs may be any that keep to these rules, and one draw needn't show every extreme that they name: `block_lists`: row b names 13 different key blocks and its first entry is block b itself; entries at or after the row's count are padding and are ignored. `block_counts`: some query block in every draw has all 13 entries valid.
All inputs are finite; a program needn't handle non-finite values.
Results may differ from the reference program's by a relative error of at most 0.0057.
Values may be sent and summed in bfloat16 or wider, within the bound.
A program may use at most 128 MiB of HBM per device.

```python
import math
import jax
import jax.numpy as jnp
from jax import lax

D = 1024
HEADS = 16
CH = 256
GRID = 32
BLOCK = 128
FRAMES = 8
BLOCKS = 64
SLOTS = 13


def draw_tokens(key, part):
    base = jax.random.fold_in(key, 101)
    shape = (FRAMES, GRID * GRID, D)
    values = jax.random.normal(base, shape, jnp.float32)
    return jnp.clip(values, -6.0, 6.0)


def draw_qkv_weight(key, part):
    base = jax.random.fold_in(key, 202)
    head_dim = D // HEADS
    values = jax.random.normal(base, (D, HEADS, 3, head_dim), jnp.float32)
    values = jnp.clip(values, -6.0, 6.0) * D ** (-0.5)
    return values.reshape(D, 3 * D)


def draw_block_lists(key, part):
    base = jax.random.fold_in(key, 303)
    row_keys = jax.random.split(base, BLOCKS)
    others = jax.vmap(lambda row_key: jax.random.permutation(row_key, BLOCKS - 1))(row_keys)
    others = others[:, :SLOTS - 1].astype(jnp.int32)
    own_block = jnp.arange(BLOCKS, dtype=jnp.int32)[:, None]
    others = others + (others >= own_block).astype(jnp.int32)
    return jnp.concatenate([own_block, others], axis=1)


def draw_block_counts(key, part):
    base = jax.random.fold_in(key, 404)
    busy_key, forced_key, count_key = jax.random.split(base, 3)
    frame_flags = jax.random.randint(busy_key, (FRAMES,), 0, 4)
    forced = jax.random.randint(forced_key, (), 0, FRAMES)
    frame_ids = jnp.arange(FRAMES, dtype=jnp.int32)
    busy = (frame_flags == 0) | (frame_ids == forced)
    busy_blocks = jnp.repeat(busy, GRID * GRID // BLOCK, total_repeat_length=BLOCKS)
    light = jax.random.randint(count_key, (BLOCKS,), 1, SLOTS // 3 + 1)
    return jnp.where(busy_blocks, SLOTS, light).astype(jnp.int32)


def scatter_about(rng, extent, scale, most, kind=jnp.bfloat16):
    entries = scale * jax.random.normal(rng, extent, jnp.float32)
    return jnp.clip(entries, min=-most, max=most).astype(kind)


def setup_inputs(seed: int = 0) -> dict:
    arg_keys = jax.random.split(jax.random.key(seed), 11)
    tokens = draw_tokens(jax.random.fold_in(arg_keys[10], 71), 0)
    qkv_weight = draw_qkv_weight(jax.random.fold_in(arg_keys[10], 71), 0)
    out_weight = scatter_about(arg_keys[2], (D, D), D ** -0.5, 0.1875, jnp.float32)
    norm_gain = jnp.clip(1.0 + 0.18 * jax.random.normal(arg_keys[3], (D,), jnp.float32), 0.1, 1.9)
    proj_weight = scatter_about(arg_keys[4], (D, CH), D ** -0.5, 0.1875, jnp.float32)
    up_weight = scatter_about(arg_keys[5], (CH, 16 * CH), CH ** -0.5, 0.375)
    conv_weight = scatter_about(arg_keys[6], (2, 3, 3, CH, CH), (9 * CH) ** -0.5, 0.125)
    conv_bias = scatter_about(arg_keys[7], (2, CH), 0.5, 3.0, jnp.float32)
    block_lists = draw_block_lists(jax.random.fold_in(arg_keys[10], 71), 0)
    block_counts = draw_block_counts(jax.random.fold_in(arg_keys[10], 71), 0)
    return dict(tokens=tokens, qkv_weight=qkv_weight, out_weight=out_weight, norm_gain=norm_gain, proj_weight=proj_weight, up_weight=up_weight, conv_weight=conv_weight, conv_bias=conv_bias, block_lists=block_lists, block_counts=block_counts)


highest = lax.Precision.HIGHEST
eps_norm = 1e-05

def attend(queries, key_values, block_ids, counts, factor):
    groups, slot_total = block_ids.shape
    block_size = queries.shape[1]
    picked = key_values[block_ids]
    picked = picked.reshape((groups, slot_total * block_size) + picked.shape[3:])
    scores = jnp.einsum('gihe,gjhe->ghij', queries, picked[:, :, :, 0, :], precision=highest) * factor
    slot_of = jnp.arange(slot_total * block_size, dtype=jnp.int32) // block_size
    usable = slot_of[None, :] < counts[:, None]
    scores = jnp.where(usable[:, None, None, :], scores, -jnp.inf)
    row_max = lax.optimization_barrier(jnp.max(scores, axis=3, keepdims=True))
    weights = jnp.exp(scores - row_max)
    totals = lax.optimization_barrier(jnp.sum(weights, axis=3))
    blended = jnp.einsum('ghij,gjhe->gihe', weights, picked[:, :, :, 1, :], precision=highest)
    return blended / jnp.transpose(totals, (0, 2, 1))[:, :, :, None]

def layer_norm(rows, gain):
    centre = lax.optimization_barrier(jnp.mean(rows, axis=-1, keepdims=True))
    centred = rows - centre
    spread = lax.optimization_barrier(jnp.mean(centred * centred, axis=-1, keepdims=True))
    return centred * lax.rsqrt(spread + eps_norm) * gain

def conv_window(padded, weight):
    frames_here, rows_in, cols_in, channels = padded.shape
    rows_out = rows_in - 2
    cols_out = cols_in - 2
    summed = jnp.zeros((frames_here * rows_out * cols_out, weight.shape[-1]), jnp.float32)
    for row_off in range(3):
        for col_off in range(3):
            window = padded[:, row_off:row_off + rows_out, col_off:col_off + cols_out, :]
            summed = summed + jnp.dot(window.reshape(-1, channels), weight[row_off, col_off], preferred_element_type=jnp.float32)
    return summed.reshape(frames_here, rows_out, cols_out, -1)

def pad_both(image):
    return jnp.pad(image, ((0, 0), (1, 1), (1, 1), (0, 0)))

def reference(tokens, qkv_weight, out_weight, norm_gain, proj_weight, up_weight, conv_weight, conv_bias, block_lists, block_counts):
    model_width = tokens.shape[2]
    head_dim = model_width // HEADS
    flat_rows = tokens.reshape(-1, model_width)
    packed = jnp.dot(flat_rows, qkv_weight, precision=highest, preferred_element_type=jnp.float32)
    packed = packed.reshape(-1, HEADS, 3, head_dim)
    queries = packed[:, :, 0, :].reshape(-1, BLOCK, HEADS, head_dim)
    key_values = packed[:, :, 1:, :].reshape(-1, BLOCK, HEADS, 2, head_dim)
    block_total = queries.shape[0]
    group_blocks = math.gcd(block_total, max(1, 512 // BLOCK))
    group_count = block_total // group_blocks
    factor = head_dim ** (-0.5)

    def one_group(items):
        return attend(items[0], key_values, items[1], items[2], factor)
    attended = lax.map(one_group, (queries.reshape(group_count, group_blocks, BLOCK, HEADS, head_dim), block_lists.reshape(group_count, group_blocks, -1), block_counts.reshape(group_count, group_blocks)))
    attended = attended.reshape(-1, model_width)
    stream = flat_rows + jnp.dot(attended, out_weight, precision=highest, preferred_element_type=jnp.float32)
    normed = layer_norm(stream, norm_gain)
    features = jnp.dot(normed, proj_weight, precision=highest, preferred_element_type=jnp.float32).astype(jnp.bfloat16)
    channels = features.shape[1]
    lifted = jnp.dot(features, up_weight, preferred_element_type=jnp.float32).astype(jnp.bfloat16)
    lifted = lifted.reshape(-1, GRID, GRID, 4, 4, channels)
    upsampled = jnp.transpose(lifted, (0, 1, 3, 2, 4, 5)).reshape(-1, 4 * GRID, 4 * GRID, channels)
    activated = jnp.maximum(upsampled, jnp.zeros((), jnp.bfloat16))
    first_conv = conv_window(pad_both(activated), conv_weight[0]) + conv_bias[0]
    hidden = jnp.maximum(first_conv, 0.0).astype(jnp.bfloat16)
    second = conv_window(pad_both(hidden), conv_weight[1]) + conv_bias[1]
    return (upsampled.astype(jnp.float32) + second).astype(jnp.bfloat16)
```

```python
import functools

import jax
import jax.numpy as jnp
from jax import lax
from jax.experimental import pallas as pl
from jax.experimental.pallas import tpu as pltpu
from jax.sharding import PartitionSpec as P

HEADS = 16
GRID = 32
BLOCK = 128
eps_norm = 1e-05
highest = lax.Precision.HIGHEST
f32 = jnp.float32
bf16 = jnp.bfloat16


def divisor_upto(count, most):
    return max(d for d in range(1, most + 1) if count % d == 0)


def split_hi_lo(value):
    hi = value.astype(bf16)
    return hi, (value - hi.astype(f32)).astype(bf16)


def mxu(a, b):
    return jnp.dot(a, b, preferred_element_type=f32)


def qkv_kernel(local_heads, head_dim, x_ref, w_ref, q_ref, kv_ref, w_hi, w_lo):
    @pl.when(pl.program_id(0) == 0)
    def _():
        hi, lo = split_hi_lo(w_ref[...])
        w_hi[...] = hi
        w_lo[...] = lo

    x_hi, x_lo = split_hi_lo(x_ref[...])
    acc = mxu(x_hi, w_lo[...]) + mxu(x_lo, w_hi[...])
    acc = acc + mxu(x_hi, w_hi[...])
    pair = 2 * head_dim
    rows = acc.shape[0]
    first = lax.broadcasted_iota(jnp.int32, (rows, pair), 1) < head_dim
    factor = head_dim ** (-0.5)
    for h in range(local_heads):
        both = acc[:, h * pair : (h + 1) * pair]
        turned = pltpu.roll(both, head_dim, 1)
        query = jnp.where(first, both, turned) * factor
        key = jnp.where(first, turned, both)
        q_hi, q_lo = split_hi_lo(query)
        k_hi, k_lo = split_hi_lo(key)
        q_ref[:, 2 * h * pair : (2 * h + 1) * pair] = q_hi
        q_ref[:, (2 * h + 1) * pair : (2 * h + 2) * pair] = q_lo
        kv_ref[:, h * pair : (h + 1) * pair] = jnp.where(first, k_hi.astype(f32), k_lo.astype(f32)).astype(bf16)
    kv_ref[:, local_heads * pair :] = acc[:, local_heads * pair :].astype(bf16)


def project(rows, weight, local_heads, head_dim):
    total, width = rows.shape
    tile = 256
    columns = weight.shape[1]
    return pl.pallas_call(
        functools.partial(qkv_kernel, local_heads, head_dim),
        grid=(total // tile,),
        in_specs=[
            pl.BlockSpec((tile, width), lambda i: (i, 0)),
            pl.BlockSpec((width, columns), lambda i: (0, 0)),
        ],
        out_specs=[
            pl.BlockSpec((tile, local_heads * 4 * head_dim), lambda i: (i, 0)),
            pl.BlockSpec((tile, columns), lambda i: (i, 0)),
        ],
        out_shape=[
            jax.ShapeDtypeStruct((total, local_heads * 4 * head_dim), bf16),
            jax.ShapeDtypeStruct((total, columns), bf16),
        ],
        scratch_shapes=[pltpu.VMEM((width, columns), bf16)] * 2,
        compiler_params=pltpu.CompilerParams(vmem_limit_bytes=48 << 20),
        name="qkv",
    )(rows, weight)


def attend_kernel(local_heads, head_dim, span, lists, counts, q_ref, kv_ref, o_ref):
    b = pl.program_id(0)
    count = counts[b]
    pair = 2 * head_dim
    v_at = local_heads * pair
    v_width = local_heads * head_dim
    stacked = [
        jnp.concatenate(
            [
                q_ref[:, 2 * h * pair : (2 * h + 1) * pair],
                q_ref[:, (2 * h + 1) * pair : (2 * h + 2) * pair],
            ],
            axis=0,
        )
        for h in range(local_heads)
    ]

    def chunk(c, carry):
        offsets = []
        valid = []
        for t in range(span):
            slot = c * span + t
            block = lists[b, jnp.minimum(slot, count - 1)]
            offsets.append(pl.multiple_of(block * BLOCK, BLOCK))
            valid.append(slot < count)
        values = jnp.concatenate(
            [kv_ref[pl.ds(at, BLOCK), v_at : v_at + v_width] for at in offsets], axis=0
        )
        out = []
        for h in range(local_heads):
            top, total, blend = carry[h]
            scores = []
            for at, ok in zip(offsets, valid):
                keys = kv_ref[pl.ds(at, BLOCK), h * pair : (h + 1) * pair]
                both = lax.dot_general(
                    stacked[h], keys, (((1,), (1,)), ((), ())), preferred_element_type=f32
                )
                scores.append(jnp.where(ok, both[:BLOCK] + both[BLOCK:], -jnp.inf))
            peak = functools.reduce(jnp.maximum, scores)
            new_top = jnp.maximum(top, jnp.max(peak, axis=1, keepdims=True))
            scale = jnp.exp(top - new_top)
            weights = [jnp.exp(s - new_top) for s in scores]
            total = total * scale + functools.reduce(jnp.add, weights)
            packed = jnp.concatenate([w.astype(bf16) for w in weights], axis=1)
            blend = blend * scale + mxu(packed, values)
            out.append((new_top, total, blend))
        return tuple(out)

    start = tuple(
        (
            jnp.full((BLOCK, 1), -jnp.inf, f32),
            jnp.zeros((BLOCK, BLOCK), f32),
            jnp.zeros((BLOCK, v_width), f32),
        )
        for _ in range(local_heads)
    )
    final = lax.fori_loop(0, (count + span - 1) // span, chunk, start)
    owner = lax.broadcasted_iota(jnp.int32, (BLOCK, v_width), 1) // head_dim
    result = jnp.zeros((BLOCK, v_width), f32)
    for h in range(local_heads):
        _, total, blend = final[h]
        ready = blend / jnp.sum(total, axis=1, keepdims=True)
        result = jnp.where(owner == h, ready, result)
    o_ref[...] = result.astype(bf16)


def attend(queries, pairs, lists, counts, local_heads, head_dim):
    blocks, slots = lists.shape
    span = -(-slots // (-(-slots // 7)))
    width = local_heads * head_dim
    return pl.pallas_call(
        functools.partial(attend_kernel, local_heads, head_dim, span),
        grid_spec=pltpu.PrefetchScalarGridSpec(
            num_scalar_prefetch=2,
            grid=(blocks,),
            in_specs=[
                pl.BlockSpec((BLOCK, queries.shape[1]), lambda i, *_: (i, 0)),
                pl.BlockSpec(pairs.shape, lambda i, *_: (0, 0), pipeline_mode=pl.Buffered(1)),
            ],
            out_specs=pl.BlockSpec((BLOCK, width), lambda i, *_: (i, 0)),
        ),
        out_shape=jax.ShapeDtypeStruct((blocks * BLOCK, width), bf16),
        compiler_params=pltpu.CompilerParams(vmem_limit_bytes=48 << 20),
        name="attend",
    )(lists, counts, queries, pairs)


def head_kernel(
    token_rows, place, feat_ref, up_ref, conv_ref, bias_ref, out_ref, up_map, act_map, hid_map, flat
):
    channels = feat_ref.shape[-1]
    ext = token_rows + 2
    pixel_cols = 4 * GRID
    feat = feat_ref[0]
    for a in range(4):
        for e in range(4):
            at = (4 * a + e) * channels
            lifted = mxu(feat, up_ref[:, at : at + channels]).astype(bf16)
            for r in range(ext):
                piece = lifted[r * GRID : (r + 1) * GRID]
                up_map[4 * r + a, e * GRID : (e + 1) * GRID, :] = piece
                act_map[4 * r + a, e * GRID : (e + 1) * GRID, :] = jnp.maximum(
                    piece, jnp.zeros((), bf16)
                )

    def conv_rows(source, first, rows, which):
        taps = jnp.concatenate(
            [
                source[pl.ds(first + dy, rows)].reshape(rows * pixel_cols, channels)
                for dy in range(3)
            ],
            axis=1,
        )
        part = []
        for dx in range(3):
            weight = jnp.concatenate([conv_ref[which, dy, dx] for dy in range(3)], axis=0)
            part.append(mxu(taps, weight).reshape(rows, 4, GRID, channels))
        column = lax.broadcasted_iota(jnp.int32, (rows * GRID, channels), 0) % GRID

        def moved(block, step):
            block = block.reshape(rows * GRID, channels)
            turned = pltpu.roll(block, step % (rows * GRID), 0)
            rim = 0 if step > 0 else GRID - 1
            return jnp.where(column == rim, 0.0, turned).reshape(rows, GRID, channels)

        left, centre, right = part
        shifted = []
        for e in range(4):
            low = left[:, e - 1] if e > 0 else moved(left[:, 3], 1)
            high = right[:, e + 1] if e < 3 else moved(right[:, 0], -1)
            shifted.append(low + centre[:, e] + high + bias_ref[which][None, None, :])
        return shifted

    hidden_rows = 4 * token_rows + 2
    group = divisor_upto(hidden_rows, 6)
    top = place[0] == 0
    bottom = place[0] == place[1] - 1
    for g in range(hidden_rows // group):
        pieces = conv_rows(act_map, g * group + 2, group, 0)
        for e in range(4):
            value = jnp.maximum(pieces[e], 0.0).astype(bf16)
            hid_map[g * group : (g + 1) * group, e * GRID : (e + 1) * GRID, :] = value

    @pl.when(top)
    def _():
        hid_map[0] = jnp.zeros((pixel_cols, channels), bf16)

    @pl.when(bottom)
    def _():
        hid_map[hidden_rows - 1] = jnp.zeros((pixel_cols, channels), bf16)

    out_rows = 4 * token_rows
    group2 = divisor_upto(out_rows, 4)
    lanes = 128
    for g in range(out_rows // group2):
        pieces = conv_rows(hid_map, g * group2, group2, 1)
        for r in range(group2):
            y = g * group2 + r
            for e in range(4):
                value = pieces[e][r] + up_map[y + 4, e * GRID : (e + 1) * GRID, :].astype(f32)
                for n in range(channels // lanes):
                    flat[y % 2, n, pl.ds(e, GRID, stride=4), :] = value[:, n * lanes : (n + 1) * lanes]
            for n in range(channels // lanes):
                out_ref[0, y, :, n * lanes : (n + 1) * lanes] = flat[y % 2, n].astype(bf16)


def predict(features, up_weight, conv_weight, conv_bias, place, token_rows):
    frames, ext_tokens, channels = features.shape
    pixel_rows, pixel_cols = 4 * token_rows, 4 * GRID
    once = pl.Buffered(1)
    return pl.pallas_call(
        functools.partial(head_kernel, token_rows),
        grid_spec=pltpu.PrefetchScalarGridSpec(
            num_scalar_prefetch=1,
            grid=(frames,),
            in_specs=[
                pl.BlockSpec((1, ext_tokens, channels), lambda i, *_: (i, 0, 0)),
                pl.BlockSpec(up_weight.shape, lambda i, *_: (0, 0), pipeline_mode=once),
                pl.BlockSpec(conv_weight.shape, lambda i, *_: (0, 0, 0, 0, 0), pipeline_mode=once),
                pl.BlockSpec(conv_bias.shape, lambda i, *_: (0, 0), pipeline_mode=once),
            ],
            out_specs=pl.BlockSpec(
                (1, pixel_rows, pixel_cols, channels), lambda i, *_: (i, 0, 0, 0)
            ),
            scratch_shapes=[
                pltpu.VMEM((pixel_rows + 8, pixel_cols, channels), bf16),
                pltpu.VMEM((pixel_rows + 8, pixel_cols, channels), bf16),
                pltpu.VMEM((pixel_rows + 2, pixel_cols, channels), bf16),
                pltpu.VMEM((2, channels // 128, pixel_cols, 128), f32),
            ],
        ),
        out_shape=jax.ShapeDtypeStruct((frames, pixel_rows, pixel_cols, channels), bf16),
        compiler_params=pltpu.CompilerParams(vmem_limit_bytes=56 << 20),
        name="head",
    )(place, features, up_weight, conv_weight, conv_bias)


def layer_norm(rows, gain):
    centre = jnp.mean(rows, axis=-1, keepdims=True)
    centred = rows - centre
    spread = jnp.mean(centred * centred, axis=-1, keepdims=True)
    return centred * lax.rsqrt(spread + eps_norm) * gain


def local_columns(qkv_weight, local_heads, head_dim):
    width = local_heads * 3 * head_dim
    columns = lax.dynamic_slice_in_dim(qkv_weight, lax.axis_index("head") * width, width, 1)
    columns = columns.reshape(-1, local_heads, 3 * head_dim)
    pairs = columns[:, :, : 2 * head_dim].reshape(-1, local_heads * 2 * head_dim)
    values = columns[:, :, 2 * head_dim :].reshape(-1, local_heads * head_dim)
    return jnp.concatenate([pairs, values], axis=1)


def on_device(
    tokens,
    qkv_weight,
    out_weight,
    norm_gain,
    proj_weight,
    up_weight,
    conv_weight,
    conv_bias,
    block_lists,
    block_counts,
):
    local_frames, strip_tokens, model_width = tokens.shape
    head_groups = lax.axis_size("head")
    local_heads = HEADS // head_groups
    head_dim = model_width // HEADS
    frame_tokens = strip_tokens * head_groups
    weight = local_columns(qkv_weight, local_heads, head_dim)
    rows = lax.all_gather(tokens, "head", axis=1, tiled=True).reshape(-1, model_width)
    queries, own_pairs = project(rows, weight, local_heads, head_dim)
    all_pairs = lax.all_gather(own_pairs, "frame", axis=0, tiled=True)
    attended = attend(queries, all_pairs, block_lists, block_counts, local_heads, head_dim)
    attended = attended.reshape(local_frames, head_groups, strip_tokens, local_heads * head_dim)
    attended = lax.all_to_all(attended, "head", split_axis=1, concat_axis=3, tiled=True)
    attended = attended.reshape(-1, model_width)
    stream = tokens.reshape(-1, model_width) + jnp.dot(
        attended.astype(f32), out_weight, precision=highest, preferred_element_type=f32
    )
    normed = layer_norm(stream, norm_gain)
    features = jnp.dot(
        normed, proj_weight, precision=highest, preferred_element_type=f32
    ).astype(bf16)
    channels = features.shape[1]
    features = features.reshape(local_frames, strip_tokens, channels)
    forward = [(i, i + 1) for i in range(head_groups - 1)]
    backward = [(i + 1, i) for i in range(head_groups - 1)]
    above = lax.ppermute(features[:, strip_tokens - GRID :], "head", forward)
    below = lax.ppermute(features[:, :GRID], "head", backward)
    extended = jnp.concatenate([above, features, below], axis=1)
    place = jnp.stack(
        [lax.axis_index("head").astype(jnp.int32), jnp.full((), head_groups, jnp.int32)]
    )
    return predict(extended, up_weight, conv_weight, conv_bias, place, strip_tokens // GRID)


def solution(mesh):
    in_specs = (
        P("frame", "head", None),
        P(),
        P(),
        P(),
        P(),
        P(),
        P(),
        P(),
        P("frame", None),
        P("frame"),
    )
    out_specs = P("frame", "head", None, None)
    return jax.shard_map(
        on_device, mesh=mesh, in_specs=in_specs, out_specs=out_specs, check_vma=False
    )
```

```python
import functools

import jax
import jax.numpy as jnp
from jax import lax
from jax.experimental import pallas as pl
from jax.experimental.pallas import tpu as pltpu
from jax.sharding import PartitionSpec as P

HEADS = 16
GRID = 32
BLOCK = 128
eps_norm = 1e-05
highest = lax.Precision.HIGHEST
f32 = jnp.float32
bf16 = jnp.bfloat16


def divisor_upto(count, most):
    return max(d for d in range(1, most + 1) if count % d == 0)


def split_hi_lo(value):
    hi = value.astype(bf16)
    return hi, (value - hi.astype(f32)).astype(bf16)


def mxu(a, b):
    return jnp.dot(a, b, preferred_element_type=f32)


def qkv_kernel(local_heads, head_dim, x_ref, w_ref, q_ref, kv_ref, x_hi, x_lo):
    @pl.when(pl.program_id(0) == 0)
    def _():
        hi, lo = split_hi_lo(x_ref[...])
        x_hi[...] = hi
        x_lo[...] = lo

    w_hi, w_lo = split_hi_lo(w_ref[...])
    acc = mxu(x_hi[...], w_lo) + mxu(x_lo[...], w_hi)
    acc = acc + mxu(x_hi[...], w_hi)
    pair = 2 * head_dim
    frames, _, strip, _ = q_ref.shape
    rows = frames * strip
    first = lax.broadcasted_iota(jnp.int32, (rows, pair), 1) < head_dim
    parts = [acc[:, n * pair : (n + 1) * pair] for n in range(3)]
    turned = [pltpu.roll(part, head_dim, 1) for part in parts]

    def coded(value):
        rest = value - value.astype(bf16).astype(f32)
        return jnp.where(first, value, rest).astype(bf16).reshape(frames, strip, pair)

    factor = head_dim ** (-0.5)
    queries = [
        coded(jnp.where(first, parts[0], turned[0]) * factor),
        coded(jnp.where(first, turned[1], parts[1]) * factor),
    ]
    keys = [
        coded(jnp.where(first, turned[0], parts[0])),
        coded(jnp.where(first, parts[2], turned[2])),
    ]
    if local_heads == 2:
        for h in range(2):
            q_ref[:, 0, :, h * pair : (h + 1) * pair] = queries[h]
            kv_ref[:, 0, :, h * pair : (h + 1) * pair] = keys[h]
        values = jnp.where(first, parts[1], parts[2]).astype(bf16)
        kv_ref[:, 0, :, 2 * pair :] = values.reshape(frames, strip, pair)
    else:
        for h, values in enumerate((parts[1], turned[2])):
            q_ref[:, h] = queries[h]
            kv_ref[:, h, :, :pair] = keys[h]
            values = values[:, :head_dim].astype(bf16)
            kv_ref[:, h, :, pair:] = values.reshape(frames, strip, head_dim)


def project(tokens, weight, head_groups, head_dim):
    frames, strip, width = tokens.shape
    local_heads = HEADS // head_groups
    share = 2 // local_heads
    columns = 6 * head_dim
    q_width, kv_width = local_heads * 2 * head_dim, local_heads * 3 * head_dim
    return pl.pallas_call(
        functools.partial(qkv_kernel, local_heads, head_dim),
        grid=(HEADS // 2,),
        in_specs=[
            pl.BlockSpec((frames * strip, width), lambda i: (0, 0)),
            pl.BlockSpec((width, columns), lambda i: (0, i)),
        ],
        out_specs=[
            pl.BlockSpec((frames, share, strip, q_width), lambda i: (0, i, 0, 0)),
            pl.BlockSpec((frames, share, strip, kv_width), lambda i: (0, i, 0, 0)),
        ],
        out_shape=[
            jax.ShapeDtypeStruct((frames, head_groups, strip, q_width), bf16),
            jax.ShapeDtypeStruct((frames, head_groups, strip, kv_width), bf16),
        ],
        scratch_shapes=[pltpu.VMEM((frames * strip, width), bf16)] * 2,
        compiler_params=pltpu.CompilerParams(vmem_limit_bytes=48 << 20),
        name="qkv",
    )(tokens.reshape(-1, width), weight)


MESH = pl.DeviceIdType.MESH


def near_first(count):
    return sorted(range(1, count), key=lambda j: (min(j, count - j), j))


def greet(peers):
    barrier = pltpu.get_barrier_semaphore()
    for peer in peers:
        pl.semaphore_signal(barrier, inc=1, device_id=peer, device_id_type=MESH)
    pl.semaphore_wait(barrier, len(peers))


def exchange_kernel(
    groups, teams, q_ref, kv_ref, q_out, pairs, own_sem,
    q_send, q_recv, z_send, z_recv, f_send, f_recv, r_send, r_recv,
):
    frames = q_ref.shape[0]
    team, me = lax.axis_index("frame"), lax.axis_index("head")
    square = teams == 4
    if square:
        side = lax.rem(team, 2)
        beside, across = team + 1 - 2 * side, lax.rem(team + 2, 4)
        direct = [(beside, beside), (across, across)]
    else:
        direct = [
            (lax.rem(team + k, teams), lax.rem(team + teams - k, teams)) for k in range(1, teams)
        ]
    order = near_first(groups)
    peers = [(team, lax.rem(me + j, groups)) for j in order] + [(to, me) for to, _ in direct]
    greet(peers)

    def remote(src, dst, send, recv, target):
        return pltpu.make_async_remote_copy(
            src_ref=src, dst_ref=dst, send_sem=send, recv_sem=recv,
            device_id=target, device_id_type=MESH,
        )

    def z_copy(f, j):
        to = lax.rem(me + j, groups)
        return remote(
            kv_ref.at[f, to], pairs.at[team * frames + f, me],
            z_send.at[f, j], z_recv.at[f, j], (team, to),
        )

    def q_copy(f, j):
        to = lax.rem(me + j, groups)
        return remote(
            q_ref.at[f, to], q_out.at[f, me], q_send.at[f, j], q_recv.at[f, j], (team, to)
        )

    def piece(owner, f, j):
        return pairs.at[owner * frames + f, lax.rem(me + groups - j, groups)]

    def f_copy(k, f, j):
        src = kv_ref.at[f, me] if j == 0 else piece(team, f, j)
        return remote(
            src, piece(team, f, j), f_send.at[k, f, j], f_recv.at[k, f, j], (direct[k][0], me)
        )

    def r_copy(f, j):
        origin, to = (beside, across) if f % 2 == 0 else (across, beside)
        here = piece(origin, f, j)
        return remote(here, here, r_send.at[f, j], r_recv.at[f, j], (to, me))

    own = []
    for f in range(frames):
        own.append(
            pltpu.make_async_copy(kv_ref.at[f, me], pairs.at[team * frames + f, me], own_sem.at[0, f])
        )
        own.append(pltpu.make_async_copy(q_ref.at[f, me], q_out.at[f, me], own_sem.at[1, f]))
    schedule = [(f, j) for j in [0] + order for f in range(frames)]
    for f, j in schedule:
        if j:
            z_copy(f, j).start()
    for f, j in schedule:
        if j:
            q_copy(f, j).start()
    for copy in own:
        copy.start()
    lag = 2 * frames
    for n in range(len(schedule) + lag):
        if n < len(schedule):
            f, j = schedule[n]
            if j:
                z_copy(f, j).wait_recv()
            for k in range(len(direct)):
                f_copy(k, f, j).start()
        if n >= lag and square:
            f, j = schedule[n - lag]
            f_copy(f % 2, f, j).wait_recv()
            r_copy(f, j).start()
    for f, j in schedule:
        for k in range(len(direct)):
            f_copy(k, f, j).wait_send()
            if not (square and k == f % 2):
                f_copy(k, f, j).wait_recv()
        if square:
            r_copy(f, j).wait()
        if j:
            z_copy(f, j).wait_send()
            q_copy(f, j).wait()
    for copy in own:
        copy.wait()


def exchange(queries, own_pairs, groups, teams):
    frames = queries.shape[0]
    sems = lambda *shape: pltpu.SemaphoreType.DMA(shape)
    hops = 2 if teams == 4 else teams - 1
    vmem = pl.BlockSpec(memory_space=pltpu.VMEM)
    anywhere = pl.BlockSpec(memory_space=pl.ANY)
    return pl.pallas_call(
        functools.partial(exchange_kernel, groups, teams),
        in_specs=[vmem, vmem],
        out_specs=[anywhere, anywhere],
        out_shape=[
            jax.ShapeDtypeStruct(queries.shape, bf16),
            jax.ShapeDtypeStruct((teams * frames,) + own_pairs.shape[1:], bf16),
        ],
        scratch_shapes=[sems(2, frames)]
        + [sems(frames, groups)] * 4
        + [sems(hops, frames, groups)] * 2
        + [sems(frames, groups)] * 2,
        compiler_params=pltpu.CompilerParams(collective_id=0, has_side_effects=True),
        name="exchange",
    )(queries, own_pairs)


def hand_back_kernel(groups, src, dst, own_sem, send, recv):
    team, me = lax.axis_index("frame"), lax.axis_index("head")
    order = near_first(groups)
    greet([(team, lax.rem(me + j, groups)) for j in order])
    copies = []
    for j in reversed(order):
        to = lax.rem(me + j, groups)
        copies.append(
            pltpu.make_async_remote_copy(
                src_ref=src.at[:, to], dst_ref=dst.at[me],
                send_sem=send.at[j], recv_sem=recv.at[j],
                device_id=(team, to), device_id_type=MESH,
            )
        )
    copies.append(pltpu.make_async_copy(src.at[:, me], dst.at[me], own_sem))
    for copy in copies:
        copy.start()
    for copy in copies:
        copy.wait()


def hand_back(attended):
    frames, groups, strip, width = attended.shape
    vmem = pl.BlockSpec(memory_space=pltpu.VMEM)
    return pl.pallas_call(
        functools.partial(hand_back_kernel, groups),
        in_specs=[vmem],
        out_specs=vmem,
        out_shape=jax.ShapeDtypeStruct((groups, frames, strip, width), bf16),
        scratch_shapes=[pltpu.SemaphoreType.DMA] + [pltpu.SemaphoreType.DMA((groups,))] * 2,
        compiler_params=pltpu.CompilerParams(collective_id=1, has_side_effects=True),
        name="hand_back",
    )(attended)


def attend_kernel(local_heads, head_dim, span, lists, counts, q_ref, kv_ref, o_ref):
    b = pl.program_id(0)
    count = counts[b]
    pair = 2 * head_dim
    v_at = local_heads * pair
    v_width = local_heads * head_dim
    first = lax.broadcasted_iota(jnp.int32, (BLOCK, pair), 1) < head_dim
    stacked = []
    for h in range(local_heads):
        coded = q_ref[:, h * pair : (h + 1) * pair].astype(f32)
        turned = pltpu.roll(coded, head_dim, 1)
        high, low = jnp.where(first, coded, turned), jnp.where(first, turned, coded)
        stacked.append(jnp.concatenate([high, low], axis=0).astype(bf16))

    def chunk(c, carry):
        offsets = []
        valid = []
        for t in range(span):
            slot = c * span + t
            block = lists[b, jnp.minimum(slot, count - 1)]
            offsets.append(pl.multiple_of(block * BLOCK, BLOCK))
            valid.append(slot < count)
        values = jnp.concatenate(
            [kv_ref[pl.ds(at, BLOCK), v_at : v_at + v_width] for at in offsets], axis=0
        )
        out = []
        for h in range(local_heads):
            top, total, blend = carry[h]
            scores = []
            for at, ok in zip(offsets, valid):
                keys = kv_ref[pl.ds(at, BLOCK), h * pair : (h + 1) * pair]
                both = lax.dot_general(
                    stacked[h], keys, (((1,), (1,)), ((), ())), preferred_element_type=f32
                )
                scores.append(jnp.where(ok, both[:BLOCK] + both[BLOCK:], -jnp.inf))
            peak = functools.reduce(jnp.maximum, scores)
            new_top = jnp.maximum(top, jnp.max(peak, axis=1, keepdims=True))
            scale = jnp.exp(top - new_top)
            weights = [jnp.exp(s - new_top) for s in scores]
            total = total * scale + functools.reduce(jnp.add, weights)
            packed = jnp.concatenate([w.astype(bf16) for w in weights], axis=1)
            blend = blend * scale + mxu(packed, values)
            out.append((new_top, total, blend))
        return tuple(out)

    start = tuple(
        (
            jnp.full((BLOCK, 1), -jnp.inf, f32),
            jnp.zeros((BLOCK, BLOCK), f32),
            jnp.zeros((BLOCK, v_width), f32),
        )
        for _ in range(local_heads)
    )
    final = lax.fori_loop(0, (count + span - 1) // span, chunk, start)
    owner = lax.broadcasted_iota(jnp.int32, (BLOCK, v_width), 1) // head_dim
    result = jnp.zeros((BLOCK, v_width), f32)
    for h in range(local_heads):
        _, total, blend = final[h]
        ready = blend / jnp.sum(total, axis=1, keepdims=True)
        result = jnp.where(owner == h, ready, result)
    o_ref[...] = result.astype(bf16)


def attend(queries, pairs, lists, counts, local_heads, head_dim):
    blocks, slots = lists.shape
    span = -(-slots // (-(-slots // 7)))
    width = local_heads * head_dim
    return pl.pallas_call(
        functools.partial(attend_kernel, local_heads, head_dim, span),
        grid_spec=pltpu.PrefetchScalarGridSpec(
            num_scalar_prefetch=2,
            grid=(blocks,),
            in_specs=[
                pl.BlockSpec((BLOCK, queries.shape[1]), lambda i, *_: (i, 0)),
                pl.BlockSpec(pairs.shape, lambda i, *_: (0, 0), pipeline_mode=pl.Buffered(1)),
            ],
            out_specs=pl.BlockSpec((BLOCK, width), lambda i, *_: (i, 0)),
        ),
        out_shape=jax.ShapeDtypeStruct((blocks * BLOCK, width), bf16),
        compiler_params=pltpu.CompilerParams(vmem_limit_bytes=48 << 20),
        name="attend",
    )(lists, counts, queries, pairs)


def head_kernel(
    token_rows, place, feat_ref, up_ref, conv_ref, bias_ref, out_ref, up_map, act_map, hid_map, flat
):
    channels = feat_ref.shape[-1]
    ext = token_rows + 2
    pixel_cols = 4 * GRID
    feat = feat_ref[0]
    for a in range(4):
        for e in range(4):
            at = (4 * a + e) * channels
            lifted = mxu(feat, up_ref[:, at : at + channels]).astype(bf16)
            for r in range(ext):
                piece = lifted[r * GRID : (r + 1) * GRID]
                up_map[4 * r + a, e * GRID : (e + 1) * GRID, :] = piece
                act_map[4 * r + a, e * GRID : (e + 1) * GRID, :] = jnp.maximum(
                    piece, jnp.zeros((), bf16)
                )

    def conv_rows(source, first, rows, which):
        taps = jnp.concatenate(
            [
                source[pl.ds(first + dy, rows)].reshape(rows * pixel_cols, channels)
                for dy in range(3)
            ],
            axis=1,
        )
        part = []
        for dx in range(3):
            weight = jnp.concatenate([conv_ref[which, dy, dx] for dy in range(3)], axis=0)
            part.append(mxu(taps, weight).reshape(rows, 4, GRID, channels))
        column = lax.broadcasted_iota(jnp.int32, (rows * GRID, channels), 0) % GRID

        def moved(block, step):
            block = block.reshape(rows * GRID, channels)
            turned = pltpu.roll(block, step % (rows * GRID), 0)
            rim = 0 if step > 0 else GRID - 1
            return jnp.where(column == rim, 0.0, turned).reshape(rows, GRID, channels)

        left, centre, right = part
        shifted = []
        for e in range(4):
            low = left[:, e - 1] if e > 0 else moved(left[:, 3], 1)
            high = right[:, e + 1] if e < 3 else moved(right[:, 0], -1)
            shifted.append(low + centre[:, e] + high + bias_ref[which][None, None, :])
        return shifted

    hidden_rows = 4 * token_rows + 2
    group = divisor_upto(hidden_rows, 6)
    top = place[0] == 0
    bottom = place[0] == place[1] - 1
    for g in range(hidden_rows // group):
        pieces = conv_rows(act_map, g * group + 2, group, 0)
        for e in range(4):
            value = jnp.maximum(pieces[e], 0.0).astype(bf16)
            hid_map[g * group : (g + 1) * group, e * GRID : (e + 1) * GRID, :] = value

    @pl.when(top)
    def _():
        hid_map[0] = jnp.zeros((pixel_cols, channels), bf16)

    @pl.when(bottom)
    def _():
        hid_map[hidden_rows - 1] = jnp.zeros((pixel_cols, channels), bf16)

    out_rows = 4 * token_rows
    group2 = divisor_upto(out_rows, 4)
    lanes = 128
    for g in range(out_rows // group2):
        pieces = conv_rows(hid_map, g * group2, group2, 1)
        for r in range(group2):
            y = g * group2 + r
            for e in range(4):
                value = pieces[e][r] + up_map[y + 4, e * GRID : (e + 1) * GRID, :].astype(f32)
                for n in range(channels // lanes):
                    flat[y % 2, n, pl.ds(e, GRID, stride=4), :] = value[:, n * lanes : (n + 1) * lanes]
            for n in range(channels // lanes):
                out_ref[0, y, :, n * lanes : (n + 1) * lanes] = flat[y % 2, n].astype(bf16)


def predict(features, up_weight, conv_weight, conv_bias, place, token_rows):
    frames, ext_tokens, channels = features.shape
    pixel_rows, pixel_cols = 4 * token_rows, 4 * GRID
    once = pl.Buffered(1)
    return pl.pallas_call(
        functools.partial(head_kernel, token_rows),
        grid_spec=pltpu.PrefetchScalarGridSpec(
            num_scalar_prefetch=1,
            grid=(frames,),
            in_specs=[
                pl.BlockSpec((1, ext_tokens, channels), lambda i, *_: (i, 0, 0)),
                pl.BlockSpec(up_weight.shape, lambda i, *_: (0, 0), pipeline_mode=once),
                pl.BlockSpec(conv_weight.shape, lambda i, *_: (0, 0, 0, 0, 0), pipeline_mode=once),
                pl.BlockSpec(conv_bias.shape, lambda i, *_: (0, 0), pipeline_mode=once),
            ],
            out_specs=pl.BlockSpec(
                (1, pixel_rows, pixel_cols, channels), lambda i, *_: (i, 0, 0, 0)
            ),
            scratch_shapes=[
                pltpu.VMEM((pixel_rows + 8, pixel_cols, channels), bf16),
                pltpu.VMEM((pixel_rows + 8, pixel_cols, channels), bf16),
                pltpu.VMEM((pixel_rows + 2, pixel_cols, channels), bf16),
                pltpu.VMEM((2, channels // 128, pixel_cols, 128), f32),
            ],
        ),
        out_shape=jax.ShapeDtypeStruct((frames, pixel_rows, pixel_cols, channels), bf16),
        compiler_params=pltpu.CompilerParams(vmem_limit_bytes=56 << 20),
        name="head",
    )(place, features, up_weight, conv_weight, conv_bias)


def layer_norm(rows, gain):
    centre = jnp.mean(rows, axis=-1, keepdims=True)
    centred = rows - centre
    spread = jnp.mean(centred * centred, axis=-1, keepdims=True)
    return centred * lax.rsqrt(spread + eps_norm) * gain


def on_device(
    tokens,
    qkv_weight,
    out_weight,
    norm_gain,
    proj_weight,
    up_weight,
    conv_weight,
    conv_bias,
    block_lists,
    block_counts,
):
    local_frames, strip_tokens, model_width = tokens.shape
    head_groups = lax.axis_size("head")
    local_heads = HEADS // head_groups
    head_dim = model_width // HEADS
    own_queries, own_pairs = project(tokens, qkv_weight, head_groups, head_dim)
    queries, all_pairs = exchange(own_queries, own_pairs, head_groups, lax.axis_size("frame"))
    queries = queries.reshape(-1, queries.shape[-1])
    all_pairs = all_pairs.reshape(-1, all_pairs.shape[-1])
    attended = attend(queries, all_pairs, block_lists, block_counts, local_heads, head_dim)
    attended = attended.reshape(local_frames, head_groups, strip_tokens, local_heads * head_dim)
    attended = hand_back(attended).reshape(head_groups, -1, local_heads * head_dim)
    attended = jnp.transpose(attended, (1, 0, 2)).reshape(-1, model_width)
    stream = tokens.reshape(-1, model_width) + jnp.dot(
        attended.astype(f32), out_weight, precision=highest, preferred_element_type=f32
    )
    normed = layer_norm(stream, norm_gain)
    features = jnp.dot(
        normed, proj_weight, precision=highest, preferred_element_type=f32
    ).astype(bf16)
    channels = features.shape[1]
    features = features.reshape(local_frames, strip_tokens, channels)
    forward = [(i, i + 1) for i in range(head_groups - 1)]
    backward = [(i + 1, i) for i in range(head_groups - 1)]
    above = lax.ppermute(features[:, strip_tokens - GRID :], "head", forward)
    below = lax.ppermute(features[:, :GRID], "head", backward)
    extended = jnp.concatenate([above, features, below], axis=1)
    place = jnp.stack(
        [lax.axis_index("head").astype(jnp.int32), jnp.full((), head_groups, jnp.int32)]
    )
    return predict(extended, up_weight, conv_weight, conv_bias, place, strip_tokens // GRID)


def solution(mesh):
    in_specs = (
        P("frame", "head", None),
        P(),
        P(),
        P(),
        P(),
        P(),
        P(),
        P(),
        P("frame", None),
        P("frame"),
    )
    out_specs = P("frame", "head", None, None)
    return jax.shard_map(
        on_device, mesh=mesh, in_specs=in_specs, out_specs=out_specs, check_vma=False
    )
```

```python
import functools

import jax
import jax.numpy as jnp
from jax import lax
from jax.experimental import pallas as pl
from jax.experimental.pallas import tpu as pltpu
from jax.sharding import PartitionSpec as P

HEADS = 16
GRID = 32
BLOCK = 128
eps_norm = 1e-05
highest = lax.Precision.HIGHEST
f32 = jnp.float32
bf16 = jnp.bfloat16


def divisor_upto(count, most):
    return max(d for d in range(1, most + 1) if count % d == 0)


def split_hi_lo(value):
    hi = value.astype(bf16)
    return hi, (value - hi.astype(f32)).astype(bf16)


def mxu(a, b):
    return jnp.dot(a, b, preferred_element_type=f32)


def qkv_kernel(local_heads, head_dim, x_ref, w_ref, q_ref, kv_ref, x_hi, x_lo):
    @pl.when(pl.program_id(0) == 0)
    def _():
        hi, lo = split_hi_lo(x_ref[...])
        x_hi[...] = hi
        x_lo[...] = lo

    w_hi, w_lo = split_hi_lo(w_ref[...])
    acc = mxu(x_hi[...], w_lo) + mxu(x_lo[...], w_hi)
    acc = acc + mxu(x_hi[...], w_hi)
    pair = 2 * head_dim
    frames, _, strip, _ = q_ref.shape
    rows = frames * strip
    first = lax.broadcasted_iota(jnp.int32, (rows, pair), 1) < head_dim
    parts = [acc[:, n * pair : (n + 1) * pair] for n in range(3)]
    turned = [pltpu.roll(part, head_dim, 1) for part in parts]

    def coded(value):
        rest = value - value.astype(bf16).astype(f32)
        return jnp.where(first, value, rest).astype(bf16).reshape(frames, strip, pair)

    factor = head_dim ** (-0.5)
    queries = [
        coded(jnp.where(first, parts[0], turned[0]) * factor),
        coded(jnp.where(first, turned[1], parts[1]) * factor),
    ]
    keys = [
        coded(jnp.where(first, turned[0], parts[0])),
        coded(jnp.where(first, parts[2], turned[2])),
    ]
    if local_heads == 2:
        for h in range(2):
            q_ref[:, 0, :, h * pair : (h + 1) * pair] = queries[h]
            kv_ref[:, 0, :, h * pair : (h + 1) * pair] = keys[h]
        values = jnp.where(first, parts[1], parts[2]).astype(bf16)
        kv_ref[:, 0, :, 2 * pair :] = values.reshape(frames, strip, pair)
    else:
        for h, values in enumerate((parts[1], turned[2])):
            q_ref[:, h] = queries[h]
            kv_ref[:, h, :, :pair] = keys[h]
            values = values[:, :head_dim].astype(bf16)
            kv_ref[:, h, :, pair:] = values.reshape(frames, strip, head_dim)


def project(tokens, weight, head_groups, head_dim):
    frames, strip, width = tokens.shape
    local_heads = HEADS // head_groups
    share = 2 // local_heads
    columns = 6 * head_dim
    q_width, kv_width = local_heads * 2 * head_dim, local_heads * 3 * head_dim
    return pl.pallas_call(
        functools.partial(qkv_kernel, local_heads, head_dim),
        grid=(HEADS // 2,),
        in_specs=[
            pl.BlockSpec((frames * strip, width), lambda i: (0, 0)),
            pl.BlockSpec((width, columns), lambda i: (0, i)),
        ],
        out_specs=[
            pl.BlockSpec((frames, share, strip, q_width), lambda i: (0, i, 0, 0)),
            pl.BlockSpec((frames, share, strip, kv_width), lambda i: (0, i, 0, 0)),
        ],
        out_shape=[
            jax.ShapeDtypeStruct((frames, head_groups, strip, q_width), bf16),
            jax.ShapeDtypeStruct((frames, head_groups, strip, kv_width), bf16),
        ],
        scratch_shapes=[pltpu.VMEM((frames * strip, width), bf16)] * 2,
        compiler_params=pltpu.CompilerParams(vmem_limit_bytes=48 << 20),
        name="qkv",
    )(tokens.reshape(-1, width), weight)


MESH = pl.DeviceIdType.MESH


def near_first(count):
    return sorted(range(1, count), key=lambda j: (min(j, count - j), j))


def greet(peers):
    barrier = pltpu.get_barrier_semaphore()
    for peer in peers:
        pl.semaphore_signal(barrier, inc=1, device_id=peer, device_id_type=MESH)
    pl.semaphore_wait(barrier, len(peers))


def exchange_kernel(
    groups, teams, q_ref, kv_ref, q_out, pairs, own_sem,
    q_send, q_recv, z_send, z_recv, f_send, f_recv, r_send, r_recv,
):
    frames = q_ref.shape[0]
    team, me = lax.axis_index("frame"), lax.axis_index("head")
    square = teams == 4
    if square:
        side = lax.rem(team, 2)
        beside, across = team + 1 - 2 * side, lax.rem(team + 2, 4)
        direct = [(beside, beside), (across, across)]
    else:
        direct = [
            (lax.rem(team + k, teams), lax.rem(team + teams - k, teams)) for k in range(1, teams)
        ]
    order = near_first(groups)
    peers = [(team, lax.rem(me + j, groups)) for j in order] + [(to, me) for to, _ in direct]
    greet(peers)

    def remote(src, dst, send, recv, target):
        return pltpu.make_async_remote_copy(
            src_ref=src, dst_ref=dst, send_sem=send, recv_sem=recv,
            device_id=target, device_id_type=MESH,
        )

    def z_copy(f, j):
        to = lax.rem(me + j, groups)
        return remote(
            kv_ref.at[f, to], pairs.at[team * frames + f, me],
            z_send.at[f, j], z_recv.at[f, j], (team, to),
        )

    def q_copy(f, j):
        to = lax.rem(me + j, groups)
        return remote(
            q_ref.at[f, to], q_out.at[f, me], q_send.at[f, j], q_recv.at[f, j], (team, to)
        )

    def piece(owner, f, j):
        return pairs.at[owner * frames + f, lax.rem(me + groups - j, groups)]

    def f_copy(k, f, j):
        src = kv_ref.at[f, me] if j == 0 else piece(team, f, j)
        return remote(
            src, piece(team, f, j), f_send.at[k, f, j], f_recv.at[k, f, j], (direct[k][0], me)
        )

    def r_copy(f, j):
        origin, to = (beside, across) if f % 2 == 0 else (across, beside)
        here = piece(origin, f, j)
        return remote(here, here, r_send.at[f, j], r_recv.at[f, j], (to, me))

    own = []
    for f in range(frames):
        own.append(
            pltpu.make_async_copy(kv_ref.at[f, me], pairs.at[team * frames + f, me], own_sem.at[0, f])
        )
        own.append(pltpu.make_async_copy(q_ref.at[f, me], q_out.at[f, me], own_sem.at[1, f]))
    schedule = [(f, j) for j in [0] + order for f in range(frames)]
    for f, j in schedule:
        if j:
            z_copy(f, j).start()
    for f, j in schedule:
        if j:
            q_copy(f, j).start()
    for copy in own:
        copy.start()
    lag = 2 * frames
    for n in range(len(schedule) + lag):
        if n < len(schedule):
            f, j = schedule[n]
            if j:
                z_copy(f, j).wait_recv()
            for k in range(len(direct)):
                f_copy(k, f, j).start()
        if n >= lag and square:
            f, j = schedule[n - lag]
            f_copy(f % 2, f, j).wait_recv()
            r_copy(f, j).start()
    for f, j in schedule:
        for k in range(len(direct)):
            f_copy(k, f, j).wait_send()
            if not (square and k == f % 2):
                f_copy(k, f, j).wait_recv()
        if square:
            r_copy(f, j).wait()
        if j:
            z_copy(f, j).wait_send()
            q_copy(f, j).wait()
    for copy in own:
        copy.wait()


def exchange(queries, own_pairs, groups, teams):
    frames = queries.shape[0]
    sems = lambda *shape: pltpu.SemaphoreType.DMA(shape)
    hops = 2 if teams == 4 else teams - 1
    vmem = pl.BlockSpec(memory_space=pltpu.VMEM)
    anywhere = pl.BlockSpec(memory_space=pl.ANY)
    return pl.pallas_call(
        functools.partial(exchange_kernel, groups, teams),
        in_specs=[vmem, vmem],
        out_specs=[anywhere, anywhere],
        out_shape=[
            jax.ShapeDtypeStruct(queries.shape, bf16),
            jax.ShapeDtypeStruct((teams * frames,) + own_pairs.shape[1:], bf16),
        ],
        scratch_shapes=[sems(2, frames)]
        + [sems(frames, groups)] * 4
        + [sems(hops, frames, groups)] * 2
        + [sems(frames, groups)] * 2,
        compiler_params=pltpu.CompilerParams(collective_id=0, has_side_effects=True),
        name="exchange",
    )(queries, own_pairs)


def hand_back_kernel(groups, src, dst, own_sem, send, recv):
    team, me = lax.axis_index("frame"), lax.axis_index("head")
    order = near_first(groups)
    greet([(team, lax.rem(me + j, groups)) for j in order])
    copies = []
    for j in reversed(order):
        to = lax.rem(me + j, groups)
        copies.append(
            pltpu.make_async_remote_copy(
                src_ref=src.at[:, to], dst_ref=dst.at[me],
                send_sem=send.at[j], recv_sem=recv.at[j],
                device_id=(team, to), device_id_type=MESH,
            )
        )
    copies.append(pltpu.make_async_copy(src.at[:, me], dst.at[me], own_sem))
    for copy in copies:
        copy.start()
    for copy in copies:
        copy.wait()


def hand_back(attended):
    frames, groups, strip, width = attended.shape
    vmem = pl.BlockSpec(memory_space=pltpu.VMEM)
    return pl.pallas_call(
        functools.partial(hand_back_kernel, groups),
        in_specs=[vmem],
        out_specs=vmem,
        out_shape=jax.ShapeDtypeStruct((groups, frames, strip, width), bf16),
        scratch_shapes=[pltpu.SemaphoreType.DMA] + [pltpu.SemaphoreType.DMA((groups,))] * 2,
        compiler_params=pltpu.CompilerParams(collective_id=1, has_side_effects=True),
        name="hand_back",
    )(attended)


def attend_kernel(local_heads, head_dim, span, lists, counts, q_ref, kv_ref, o_ref):
    b = pl.program_id(0)
    count = counts[b]
    pair = 2 * head_dim
    v_at = local_heads * pair
    v_width = local_heads * head_dim
    first = lax.broadcasted_iota(jnp.int32, (BLOCK, pair), 1) < head_dim
    queries = []
    for h in range(local_heads):
        coded = q_ref[:, h * pair : (h + 1) * pair].astype(f32)
        turned = pltpu.roll(coded, head_dim, 1)
        high, low = jnp.where(first, coded, turned), jnp.where(first, turned, coded)
        queries.append(jnp.concatenate([high, low], axis=1).astype(bf16))

    def chunk(c, carry):
        offsets = []
        valid = []
        for t in range(span):
            slot = c * span + t
            block = lists[b, jnp.minimum(slot, count - 1)]
            offsets.append(pl.multiple_of(block * BLOCK, BLOCK))
            valid.append(slot < count)
        values = jnp.concatenate(
            [kv_ref[pl.ds(at, BLOCK), v_at : v_at + v_width] for at in offsets], axis=0
        )
        out = []
        for h in range(local_heads):
            top, total, blend = carry[h]
            keys = jnp.concatenate(
                [kv_ref[pl.ds(at, BLOCK), h * pair : (h + 1) * pair] for at in offsets], axis=0
            )
            found = lax.dot_general(
                queries[h],
                jnp.concatenate([keys, keys], axis=1),
                (((1,), (1,)), ((), ())),
                preferred_element_type=f32,
            )
            scores = [
                jnp.where(ok, found[:, t * BLOCK : (t + 1) * BLOCK], -jnp.inf)
                for t, ok in enumerate(valid)
            ]
            peak = functools.reduce(jnp.maximum, scores)
            new_top = jnp.maximum(top, jnp.max(peak, axis=1, keepdims=True))
            scale = jnp.exp(top - new_top)
            weights = [jnp.exp(s - new_top) for s in scores]
            total = total * scale + functools.reduce(jnp.add, weights)
            packed = jnp.concatenate([w.astype(bf16) for w in weights], axis=1)
            blend = blend * scale + mxu(packed, values)
            out.append((new_top, total, blend))
        return tuple(out)

    start = tuple(
        (
            jnp.full((BLOCK, 1), -jnp.inf, f32),
            jnp.zeros((BLOCK, BLOCK), f32),
            jnp.zeros((BLOCK, v_width), f32),
        )
        for _ in range(local_heads)
    )
    final = lax.fori_loop(0, (count + span - 1) // span, chunk, start)
    owner = lax.broadcasted_iota(jnp.int32, (BLOCK, v_width), 1) // head_dim
    result = jnp.zeros((BLOCK, v_width), f32)
    for h in range(local_heads):
        _, total, blend = final[h]
        ready = blend / jnp.sum(total, axis=1, keepdims=True)
        result = jnp.where(owner == h, ready, result)
    o_ref[...] = result.astype(bf16)


def attend(queries, pairs, lists, counts, local_heads, head_dim):
    blocks, slots = lists.shape
    span = -(-slots // (-(-slots // 7)))
    width = local_heads * head_dim
    return pl.pallas_call(
        functools.partial(attend_kernel, local_heads, head_dim, span),
        grid_spec=pltpu.PrefetchScalarGridSpec(
            num_scalar_prefetch=2,
            grid=(blocks,),
            in_specs=[
                pl.BlockSpec((BLOCK, queries.shape[1]), lambda i, *_: (i, 0)),
                pl.BlockSpec(pairs.shape, lambda i, *_: (0, 0), pipeline_mode=pl.Buffered(1)),
            ],
            out_specs=pl.BlockSpec((BLOCK, width), lambda i, *_: (i, 0)),
        ),
        out_shape=jax.ShapeDtypeStruct((blocks * BLOCK, width), bf16),
        compiler_params=pltpu.CompilerParams(vmem_limit_bytes=48 << 20),
        name="attend",
    )(lists, counts, queries, pairs)


def head_kernel(
    token_rows, place, feat_ref, up_ref, conv_ref, bias_ref, out_ref, up_map, act_map, hid_map, flat
):
    channels = feat_ref.shape[-1]
    ext = token_rows + 2
    pixel_cols = 4 * GRID
    feat = feat_ref[0]
    for a in range(4):
        for e in range(4):
            at = (4 * a + e) * channels
            lifted = mxu(feat, up_ref[:, at : at + channels]).astype(bf16)
            for r in range(ext):
                piece = lifted[r * GRID : (r + 1) * GRID]
                up_map[4 * r + a, e * GRID : (e + 1) * GRID, :] = piece
                act_map[4 * r + a, e * GRID : (e + 1) * GRID, :] = jnp.maximum(
                    piece, jnp.zeros((), bf16)
                )

    def conv_rows(source, first, rows, which):
        taps = jnp.concatenate(
            [
                source[pl.ds(first + dy, rows)].reshape(rows * pixel_cols, channels)
                for dy in range(3)
            ],
            axis=1,
        )
        part = []
        for dx in range(3):
            weight = jnp.concatenate([conv_ref[which, dy, dx] for dy in range(3)], axis=0)
            part.append(mxu(taps, weight).reshape(rows, 4, GRID, channels))
        column = lax.broadcasted_iota(jnp.int32, (rows * GRID, channels), 0) % GRID

        def moved(block, step):
            block = block.reshape(rows * GRID, channels)
            turned = pltpu.roll(block, step % (rows * GRID), 0)
            rim = 0 if step > 0 else GRID - 1
            return jnp.where(column == rim, 0.0, turned).reshape(rows, GRID, channels)

        left, centre, right = part
        shifted = []
        for e in range(4):
            low = left[:, e - 1] if e > 0 else moved(left[:, 3], 1)
            high = right[:, e + 1] if e < 3 else moved(right[:, 0], -1)
            shifted.append(low + centre[:, e] + high + bias_ref[which][None, None, :])
        return shifted

    hidden_rows = 4 * token_rows + 2
    group = divisor_upto(hidden_rows, 6)
    top = place[0] == 0
    bottom = place[0] == place[1] - 1
    for g in range(hidden_rows // group):
        pieces = conv_rows(act_map, g * group + 2, group, 0)
        for e in range(4):
            value = jnp.maximum(pieces[e], 0.0).astype(bf16)
            hid_map[g * group : (g + 1) * group, e * GRID : (e + 1) * GRID, :] = value

    @pl.when(top)
    def _():
        hid_map[0] = jnp.zeros((pixel_cols, channels), bf16)

    @pl.when(bottom)
    def _():
        hid_map[hidden_rows - 1] = jnp.zeros((pixel_cols, channels), bf16)

    out_rows = 4 * token_rows
    group2 = divisor_upto(out_rows, 4)
    lanes = 128
    for g in range(out_rows // group2):
        pieces = conv_rows(hid_map, g * group2, group2, 1)
        for r in range(group2):
            y = g * group2 + r
            for e in range(4):
                value = pieces[e][r] + up_map[y + 4, e * GRID : (e + 1) * GRID, :].astype(f32)
                for n in range(channels // lanes):
                    flat[y % 2, n, pl.ds(e, GRID, stride=4), :] = value[:, n * lanes : (n + 1) * lanes]
            for n in range(channels // lanes):
                out_ref[0, y, :, n * lanes : (n + 1) * lanes] = flat[y % 2, n].astype(bf16)


def predict(features, up_weight, conv_weight, conv_bias, place, token_rows):
    frames, ext_tokens, channels = features.shape
    pixel_rows, pixel_cols = 4 * token_rows, 4 * GRID
    once = pl.Buffered(1)
    return pl.pallas_call(
        functools.partial(head_kernel, token_rows),
        grid_spec=pltpu.PrefetchScalarGridSpec(
            num_scalar_prefetch=1,
            grid=(frames,),
            in_specs=[
                pl.BlockSpec((1, ext_tokens, channels), lambda i, *_: (i, 0, 0)),
                pl.BlockSpec(up_weight.shape, lambda i, *_: (0, 0), pipeline_mode=once),
                pl.BlockSpec(conv_weight.shape, lambda i, *_: (0, 0, 0, 0, 0), pipeline_mode=once),
                pl.BlockSpec(conv_bias.shape, lambda i, *_: (0, 0), pipeline_mode=once),
            ],
            out_specs=pl.BlockSpec(
                (1, pixel_rows, pixel_cols, channels), lambda i, *_: (i, 0, 0, 0)
            ),
            scratch_shapes=[
                pltpu.VMEM((pixel_rows + 8, pixel_cols, channels), bf16),
                pltpu.VMEM((pixel_rows + 8, pixel_cols, channels), bf16),
                pltpu.VMEM((pixel_rows + 2, pixel_cols, channels), bf16),
                pltpu.VMEM((2, channels // 128, pixel_cols, 128), f32),
            ],
        ),
        out_shape=jax.ShapeDtypeStruct((frames, pixel_rows, pixel_cols, channels), bf16),
        compiler_params=pltpu.CompilerParams(vmem_limit_bytes=56 << 20),
        name="head",
    )(place, features, up_weight, conv_weight, conv_bias)


def layer_norm(rows, gain):
    centre = jnp.mean(rows, axis=-1, keepdims=True)
    centred = rows - centre
    spread = jnp.mean(centred * centred, axis=-1, keepdims=True)
    return centred * lax.rsqrt(spread + eps_norm) * gain


def on_device(
    tokens,
    qkv_weight,
    out_weight,
    norm_gain,
    proj_weight,
    up_weight,
    conv_weight,
    conv_bias,
    block_lists,
    block_counts,
):
    local_frames, strip_tokens, model_width = tokens.shape
    head_groups = lax.axis_size("head")
    local_heads = HEADS // head_groups
    head_dim = model_width // HEADS
    own_queries, own_pairs = project(tokens, qkv_weight, head_groups, head_dim)
    queries, all_pairs = exchange(own_queries, own_pairs, head_groups, lax.axis_size("frame"))
    queries = queries.reshape(-1, queries.shape[-1])
    all_pairs = all_pairs.reshape(-1, all_pairs.shape[-1])
    attended = attend(queries, all_pairs, block_lists, block_counts, local_heads, head_dim)
    attended = attended.reshape(local_frames, head_groups, strip_tokens, local_heads * head_dim)
    attended = hand_back(attended).reshape(head_groups, -1, local_heads * head_dim)
    attended = jnp.transpose(attended, (1, 0, 2)).reshape(-1, model_width)
    stream = tokens.reshape(-1, model_width) + jnp.dot(
        attended.astype(f32), out_weight, precision=highest, preferred_element_type=f32
    )
    normed = layer_norm(stream, norm_gain)
    features = jnp.dot(
        normed, proj_weight, precision=highest, preferred_element_type=f32
    ).astype(bf16)
    channels = features.shape[1]
    features = features.reshape(local_frames, strip_tokens, channels)
    forward = [(i, i + 1) for i in range(head_groups - 1)]
    backward = [(i + 1, i) for i in range(head_groups - 1)]
    above = lax.ppermute(features[:, strip_tokens - GRID :], "head", forward)
    below = lax.ppermute(features[:, :GRID], "head", backward)
    extended = jnp.concatenate([above, features, below], axis=1)
    place = jnp.stack(
        [lax.axis_index("head").astype(jnp.int32), jnp.full((), head_groups, jnp.int32)]
    )
    return predict(extended, up_weight, conv_weight, conv_bias, place, strip_tokens // GRID)


def solution(mesh):
    in_specs = (
        P("frame", "head", None),
        P(),
        P(),
        P(),
        P(),
        P(),
        P(),
        P(),
        P("frame", None),
        P("frame"),
    )
    out_specs = P("frame", "head", None, None)
    return jax.shard_map(
        on_device, mesh=mesh, in_specs=in_specs, out_specs=out_specs, check_vma=False
    )
```

```python
import functools

import jax
import jax.numpy as jnp
from jax import lax
from jax.experimental import pallas as pl
from jax.experimental.pallas import tpu as pltpu
from jax.sharding import PartitionSpec as P

HEADS = 16
GRID = 32
BLOCK = 128
eps_norm = 1e-05
highest = lax.Precision.HIGHEST
f32 = jnp.float32
bf16 = jnp.bfloat16


def divisor_upto(count, most):
    return max(d for d in range(1, most + 1) if count % d == 0)


def split_hi_lo(value):
    hi = value.astype(bf16)
    return hi, (value - hi.astype(f32)).astype(bf16)


def mxu(a, b):
    return jnp.dot(a, b, preferred_element_type=f32)


def qkv_kernel(local_heads, head_dim, x_ref, w_ref, q_ref, kv_ref, x_hi, x_lo):
    @pl.when(pl.program_id(0) == 0)
    def _():
        hi, lo = split_hi_lo(x_ref[...])
        x_hi[...] = hi
        x_lo[...] = lo

    w_hi, w_lo = split_hi_lo(w_ref[...])
    acc = mxu(x_hi[...], w_lo) + mxu(x_lo[...], w_hi)
    acc = acc + mxu(x_hi[...], w_hi)
    pair = 2 * head_dim
    frames, _, strip, _ = q_ref.shape
    rows = frames * strip
    first = lax.broadcasted_iota(jnp.int32, (rows, pair), 1) < head_dim
    parts = [acc[:, n * pair : (n + 1) * pair] for n in range(3)]
    turned = [pltpu.roll(part, head_dim, 1) for part in parts]

    def coded(value):
        rest = value - value.astype(bf16).astype(f32)
        return jnp.where(first, value, rest).astype(bf16).reshape(frames, strip, pair)

    factor = head_dim ** (-0.5)
    queries = [
        coded(jnp.where(first, parts[0], turned[0]) * factor),
        coded(jnp.where(first, turned[1], parts[1]) * factor),
    ]
    keys = [
        coded(jnp.where(first, turned[0], parts[0])),
        coded(jnp.where(first, parts[2], turned[2])),
    ]
    if local_heads == 2:
        for h in range(2):
            q_ref[:, 0, :, h * pair : (h + 1) * pair] = queries[h]
            kv_ref[:, 0, :, h * pair : (h + 1) * pair] = keys[h]
        values = jnp.where(first, parts[1], parts[2]).astype(bf16)
        kv_ref[:, 0, :, 2 * pair :] = values.reshape(frames, strip, pair)
    else:
        for h, values in enumerate((parts[1], turned[2])):
            q_ref[:, h] = queries[h]
            kv_ref[:, h, :, :pair] = keys[h]
            values = values[:, :head_dim].astype(bf16)
            kv_ref[:, h, :, pair:] = values.reshape(frames, strip, head_dim)


def project(tokens, weight, head_groups, head_dim):
    frames, strip, width = tokens.shape
    local_heads = HEADS // head_groups
    share = 2 // local_heads
    columns = 6 * head_dim
    q_width, kv_width = local_heads * 2 * head_dim, local_heads * 3 * head_dim
    return pl.pallas_call(
        functools.partial(qkv_kernel, local_heads, head_dim),
        grid=(HEADS // 2,),
        in_specs=[
            pl.BlockSpec((frames * strip, width), lambda i: (0, 0)),
            pl.BlockSpec((width, columns), lambda i: (0, i)),
        ],
        out_specs=[
            pl.BlockSpec((frames, share, strip, q_width), lambda i: (0, i, 0, 0)),
            pl.BlockSpec((frames, share, strip, kv_width), lambda i: (0, i, 0, 0)),
        ],
        out_shape=[
            jax.ShapeDtypeStruct((frames, head_groups, strip, q_width), bf16),
            jax.ShapeDtypeStruct((frames, head_groups, strip, kv_width), bf16),
        ],
        scratch_shapes=[pltpu.VMEM((frames * strip, width), bf16)] * 2,
        compiler_params=pltpu.CompilerParams(vmem_limit_bytes=48 << 20),
        name="qkv",
    )(tokens.reshape(-1, width), weight)


MESH = pl.DeviceIdType.MESH


def near_first(count):
    return sorted(range(1, count), key=lambda j: (min(j, count - j), j))


def greet(peers):
    barrier = pltpu.get_barrier_semaphore()
    for peer in peers:
        pl.semaphore_signal(barrier, inc=1, device_id=peer, device_id_type=MESH)
    pl.semaphore_wait(barrier, len(peers))


def exchange_kernel(
    groups, teams, q_ref, kv_ref, q_out, pairs, own_sem,
    q_send, q_recv, z_send, z_recv, f_send, f_recv, r_send, r_recv,
):
    frames = q_ref.shape[0]
    team, me = lax.axis_index("frame"), lax.axis_index("head")
    square = teams == 4
    if square:
        side = lax.rem(team, 2)
        beside, across = team + 1 - 2 * side, lax.rem(team + 2, 4)
        direct = [(beside, beside), (across, across)]
    else:
        direct = [
            (lax.rem(team + k, teams), lax.rem(team + teams - k, teams)) for k in range(1, teams)
        ]
    order = near_first(groups)
    peers = [(team, lax.rem(me + j, groups)) for j in order] + [(to, me) for to, _ in direct]
    greet(peers)

    def remote(src, dst, send, recv, target):
        return pltpu.make_async_remote_copy(
            src_ref=src, dst_ref=dst, send_sem=send, recv_sem=recv,
            device_id=target, device_id_type=MESH,
        )

    def z_copy(f, j):
        to = lax.rem(me + j, groups)
        return remote(
            kv_ref.at[f, to], pairs.at[team * frames + f, me],
            z_send.at[f, j], z_recv.at[f, j], (team, to),
        )

    def q_copy(f, j):
        to = lax.rem(me + j, groups)
        return remote(
            q_ref.at[f, to], q_out.at[f, me], q_send.at[f, j], q_recv.at[f, j], (team, to)
        )

    def piece(owner, f, j):
        return pairs.at[owner * frames + f, lax.rem(me + groups - j, groups)]

    def f_copy(k, f, j):
        src = kv_ref.at[f, me] if j == 0 else piece(team, f, j)
        return remote(
            src, piece(team, f, j), f_send.at[k, f, j], f_recv.at[k, f, j], (direct[k][0], me)
        )

    def r_copy(f, j):
        origin, to = (beside, across) if f % 2 == 0 else (across, beside)
        here = piece(origin, f, j)
        return remote(here, here, r_send.at[f, j], r_recv.at[f, j], (to, me))

    own = []
    for f in range(frames):
        own.append(
            pltpu.make_async_copy(kv_ref.at[f, me], pairs.at[team * frames + f, me], own_sem.at[0, f])
        )
        own.append(pltpu.make_async_copy(q_ref.at[f, me], q_out.at[f, me], own_sem.at[1, f]))
    schedule = [(f, j) for j in [0] + order for f in range(frames)]
    for f, j in schedule:
        if j:
            z_copy(f, j).start()
    for f, j in schedule:
        if j:
            q_copy(f, j).start()
    for copy in own:
        copy.start()
    lag = 2 * frames
    for n in range(len(schedule) + lag):
        if n < len(schedule):
            f, j = schedule[n]
            if j:
                z_copy(f, j).wait_recv()
            for k in range(len(direct)):
                f_copy(k, f, j).start()
        if n >= lag and square:
            f, j = schedule[n - lag]
            f_copy(f % 2, f, j).wait_recv()
            r_copy(f, j).start()
    for f, j in schedule:
        for k in range(len(direct)):
            f_copy(k, f, j).wait_send()
            if not (square and k == f % 2):
                f_copy(k, f, j).wait_recv()
        if square:
            r_copy(f, j).wait()
        if j:
            z_copy(f, j).wait_send()
            q_copy(f, j).wait()
    for copy in own:
        copy.wait()


def exchange(queries, own_pairs, groups, teams):
    frames = queries.shape[0]
    sems = lambda *shape: pltpu.SemaphoreType.DMA(shape)
    hops = 2 if teams == 4 else teams - 1
    vmem = pl.BlockSpec(memory_space=pltpu.VMEM)
    anywhere = pl.BlockSpec(memory_space=pl.ANY)
    return pl.pallas_call(
        functools.partial(exchange_kernel, groups, teams),
        in_specs=[vmem, vmem],
        out_specs=[anywhere, anywhere],
        out_shape=[
            jax.ShapeDtypeStruct(queries.shape, bf16),
            jax.ShapeDtypeStruct((teams * frames,) + own_pairs.shape[1:], bf16),
        ],
        scratch_shapes=[sems(2, frames)]
        + [sems(frames, groups)] * 4
        + [sems(hops, frames, groups)] * 2
        + [sems(frames, groups)] * 2,
        compiler_params=pltpu.CompilerParams(collective_id=0, has_side_effects=True),
        name="exchange",
    )(queries, own_pairs)


def hand_back_kernel(groups, src, dst, own_sem, send, recv):
    team, me = lax.axis_index("frame"), lax.axis_index("head")
    order = near_first(groups)
    greet([(team, lax.rem(me + j, groups)) for j in order])
    copies = []
    for j in reversed(order):
        to = lax.rem(me + j, groups)
        copies.append(
            pltpu.make_async_remote_copy(
                src_ref=src.at[:, to], dst_ref=dst.at[me],
                send_sem=send.at[j], recv_sem=recv.at[j],
                device_id=(team, to), device_id_type=MESH,
            )
        )
    copies.append(pltpu.make_async_copy(src.at[:, me], dst.at[me], own_sem))
    for copy in copies:
        copy.start()
    for copy in copies:
        copy.wait()


def hand_back(attended):
    frames, groups, strip, width = attended.shape
    vmem = pl.BlockSpec(memory_space=pltpu.VMEM)
    return pl.pallas_call(
        functools.partial(hand_back_kernel, groups),
        in_specs=[vmem],
        out_specs=vmem,
        out_shape=jax.ShapeDtypeStruct((groups, frames, strip, width), bf16),
        scratch_shapes=[pltpu.SemaphoreType.DMA] + [pltpu.SemaphoreType.DMA((groups,))] * 2,
        compiler_params=pltpu.CompilerParams(collective_id=1, has_side_effects=True),
        name="hand_back",
    )(attended)


def attend_kernel(local_heads, head_dim, span, lists, counts, q_ref, kv_ref, o_ref, turned_v):
    b = pl.program_id(0)
    count = counts[b]
    pair = 2 * head_dim
    v_at = local_heads * pair
    v_width = local_heads * head_dim

    @pl.when(b == 0)
    def _():
        @pl.loop(0, kv_ref.shape[0] // BLOCK)
        def _(n):
            at = pl.ds(pl.multiple_of(n * BLOCK, BLOCK), BLOCK)
            values = kv_ref[at, v_at : v_at + v_width].astype(f32)
            turned_v[n] = jnp.transpose(values).astype(bf16)

    first = lax.broadcasted_iota(jnp.int32, (BLOCK, pair), 1) < head_dim
    queries = []
    for h in range(local_heads):
        coded = q_ref[:, h * pair : (h + 1) * pair].astype(f32)
        turned = pltpu.roll(coded, head_dim, 1)
        high, low = jnp.where(first, coded, turned), jnp.where(first, turned, coded)
        queries.append(jnp.transpose(jnp.concatenate([high, low], axis=1)).astype(bf16))

    def chunk(c, carry):
        blocks = []
        offsets = []
        valid = []
        for t in range(span):
            slot = c * span + t
            block = lists[b, jnp.minimum(slot, count - 1)]
            blocks.append(block)
            offsets.append(pl.multiple_of(block * BLOCK, BLOCK))
            valid.append(slot < count)
        values = jnp.concatenate([turned_v[block] for block in blocks], axis=1)
        out = []
        for h in range(local_heads):
            top, total, blend = carry[h]
            keys = jnp.concatenate(
                [kv_ref[pl.ds(at, BLOCK), h * pair : (h + 1) * pair] for at in offsets], axis=0
            )
            found = mxu(jnp.concatenate([keys, keys], axis=1), queries[h])
            scores = [
                jnp.where(ok, found[t * BLOCK : (t + 1) * BLOCK], -jnp.inf)
                for t, ok in enumerate(valid)
            ]
            peak = functools.reduce(jnp.maximum, scores)
            new_top = jnp.maximum(top, jnp.max(peak, axis=0, keepdims=True))
            scale = jnp.exp(top - new_top)
            weights = [jnp.exp(s - new_top) for s in scores]
            total = total * scale + functools.reduce(jnp.add, weights)
            packed = jnp.concatenate([w.astype(bf16) for w in weights], axis=0)
            blend = blend * scale + mxu(values, packed)
            out.append((new_top, total, blend))
        return tuple(out)

    start = tuple(
        (
            jnp.full((1, BLOCK), -jnp.inf, f32),
            jnp.zeros((BLOCK, BLOCK), f32),
            jnp.zeros((v_width, BLOCK), f32),
        )
        for _ in range(local_heads)
    )
    final = lax.fori_loop(0, (count + span - 1) // span, chunk, start)
    owner = lax.broadcasted_iota(jnp.int32, (v_width, BLOCK), 0) // head_dim
    result = jnp.zeros((v_width, BLOCK), f32)
    for h in range(local_heads):
        _, total, blend = final[h]
        ready = blend / jnp.sum(total, axis=0, keepdims=True)
        result = jnp.where(owner == h, ready, result)
    o_ref[...] = jnp.transpose(result).astype(bf16)


def attend(queries, pairs, lists, counts, local_heads, head_dim):
    blocks, slots = lists.shape
    span = -(-slots // (-(-slots // 7)))
    width = local_heads * head_dim
    return pl.pallas_call(
        functools.partial(attend_kernel, local_heads, head_dim, span),
        grid_spec=pltpu.PrefetchScalarGridSpec(
            num_scalar_prefetch=2,
            grid=(blocks,),
            in_specs=[
                pl.BlockSpec((BLOCK, queries.shape[1]), lambda i, *_: (i, 0)),
                pl.BlockSpec(pairs.shape, lambda i, *_: (0, 0), pipeline_mode=pl.Buffered(1)),
            ],
            out_specs=pl.BlockSpec((BLOCK, width), lambda i, *_: (i, 0)),
            scratch_shapes=[pltpu.VMEM((pairs.shape[0] // BLOCK, width, BLOCK), bf16)],
        ),
        out_shape=jax.ShapeDtypeStruct((blocks * BLOCK, width), bf16),
        compiler_params=pltpu.CompilerParams(vmem_limit_bytes=48 << 20),
        name="attend",
    )(lists, counts, queries, pairs)


def head_kernel(
    token_rows, place, feat_ref, up_ref, conv_ref, bias_ref, out_ref, up_map, act_map, hid_map, flat
):
    channels = feat_ref.shape[-1]
    ext = token_rows + 2
    pixel_cols = 4 * GRID
    feat = feat_ref[0]
    for a in range(4):
        for e in range(4):
            at = (4 * a + e) * channels
            lifted = mxu(feat, up_ref[:, at : at + channels]).astype(bf16)
            for r in range(ext):
                piece = lifted[r * GRID : (r + 1) * GRID]
                up_map[4 * r + a, e * GRID : (e + 1) * GRID, :] = piece
                act_map[4 * r + a, e * GRID : (e + 1) * GRID, :] = jnp.maximum(
                    piece, jnp.zeros((), bf16)
                )

    def conv_rows(source, first, rows, which):
        taps = jnp.concatenate(
            [
                source[pl.ds(first + dy, rows)].reshape(rows * pixel_cols, channels)
                for dy in range(3)
            ],
            axis=1,
        )
        part = []
        for dx in range(3):
            weight = jnp.concatenate([conv_ref[which, dy, dx] for dy in range(3)], axis=0)
            part.append(mxu(taps, weight).reshape(rows, 4, GRID, channels))
        column = lax.broadcasted_iota(jnp.int32, (rows * GRID, channels), 0) % GRID

        def moved(block, step):
            block = block.reshape(rows * GRID, channels)
            turned = pltpu.roll(block, step % (rows * GRID), 0)
            rim = 0 if step > 0 else GRID - 1
            return jnp.where(column == rim, 0.0, turned).reshape(rows, GRID, channels)

        left, centre, right = part
        shifted = []
        for e in range(4):
            low = left[:, e - 1] if e > 0 else moved(left[:, 3], 1)
            high = right[:, e + 1] if e < 3 else moved(right[:, 0], -1)
            shifted.append(low + centre[:, e] + high + bias_ref[which][None, None, :])
        return shifted

    hidden_rows = 4 * token_rows + 2
    group = divisor_upto(hidden_rows, 6)
    top = place[0] == 0
    bottom = place[0] == place[1] - 1
    for g in range(hidden_rows // group):
        pieces = conv_rows(act_map, g * group + 2, group, 0)
        for e in range(4):
            value = jnp.maximum(pieces[e], 0.0).astype(bf16)
            hid_map[g * group : (g + 1) * group, e * GRID : (e + 1) * GRID, :] = value

    @pl.when(top)
    def _():
        hid_map[0] = jnp.zeros((pixel_cols, channels), bf16)

    @pl.when(bottom)
    def _():
        hid_map[hidden_rows - 1] = jnp.zeros((pixel_cols, channels), bf16)

    out_rows = 4 * token_rows
    group2 = divisor_upto(out_rows, 4)
    lanes = 128
    for g in range(out_rows // group2):
        pieces = conv_rows(hid_map, g * group2, group2, 1)
        for r in range(group2):
            y = g * group2 + r
            for e in range(4):
                value = pieces[e][r] + up_map[y + 4, e * GRID : (e + 1) * GRID, :].astype(f32)
                for n in range(channels // lanes):
                    flat[y % 2, n, pl.ds(e, GRID, stride=4), :] = value[:, n * lanes : (n + 1) * lanes]
            for n in range(channels // lanes):
                out_ref[0, y, :, n * lanes : (n + 1) * lanes] = flat[y % 2, n].astype(bf16)


def predict(features, up_weight, conv_weight, conv_bias, place, token_rows):
    frames, ext_tokens, channels = features.shape
    pixel_rows, pixel_cols = 4 * token_rows, 4 * GRID
    once = pl.Buffered(1)
    return pl.pallas_call(
        functools.partial(head_kernel, token_rows),
        grid_spec=pltpu.PrefetchScalarGridSpec(
            num_scalar_prefetch=1,
            grid=(frames,),
            in_specs=[
                pl.BlockSpec((1, ext_tokens, channels), lambda i, *_: (i, 0, 0)),
                pl.BlockSpec(up_weight.shape, lambda i, *_: (0, 0), pipeline_mode=once),
                pl.BlockSpec(conv_weight.shape, lambda i, *_: (0, 0, 0, 0, 0), pipeline_mode=once),
                pl.BlockSpec(conv_bias.shape, lambda i, *_: (0, 0), pipeline_mode=once),
            ],
            out_specs=pl.BlockSpec(
                (1, pixel_rows, pixel_cols, channels), lambda i, *_: (i, 0, 0, 0)
            ),
            scratch_shapes=[
                pltpu.VMEM((pixel_rows + 8, pixel_cols, channels), bf16),
                pltpu.VMEM((pixel_rows + 8, pixel_cols, channels), bf16),
                pltpu.VMEM((pixel_rows + 2, pixel_cols, channels), bf16),
                pltpu.VMEM((2, channels // 128, pixel_cols, 128), f32),
            ],
        ),
        out_shape=jax.ShapeDtypeStruct((frames, pixel_rows, pixel_cols, channels), bf16),
        compiler_params=pltpu.CompilerParams(vmem_limit_bytes=56 << 20),
        name="head",
    )(place, features, up_weight, conv_weight, conv_bias)


def layer_norm(rows, gain):
    centre = jnp.mean(rows, axis=-1, keepdims=True)
    centred = rows - centre
    spread = jnp.mean(centred * centred, axis=-1, keepdims=True)
    return centred * lax.rsqrt(spread + eps_norm) * gain


def on_device(
    tokens,
    qkv_weight,
    out_weight,
    norm_gain,
    proj_weight,
    up_weight,
    conv_weight,
    conv_bias,
    block_lists,
    block_counts,
):
    local_frames, strip_tokens, model_width = tokens.shape
    head_groups = lax.axis_size("head")
    local_heads = HEADS // head_groups
    head_dim = model_width // HEADS
    own_queries, own_pairs = project(tokens, qkv_weight, head_groups, head_dim)
    queries, all_pairs = exchange(own_queries, own_pairs, head_groups, lax.axis_size("frame"))
    queries = queries.reshape(-1, queries.shape[-1])
    all_pairs = all_pairs.reshape(-1, all_pairs.shape[-1])
    attended = attend(queries, all_pairs, block_lists, block_counts, local_heads, head_dim)
    attended = attended.reshape(local_frames, head_groups, strip_tokens, local_heads * head_dim)
    attended = hand_back(attended).reshape(head_groups, -1, local_heads * head_dim)
    attended = jnp.transpose(attended, (1, 0, 2)).reshape(-1, model_width)
    stream = tokens.reshape(-1, model_width) + jnp.dot(
        attended.astype(f32), out_weight, precision=highest, preferred_element_type=f32
    )
    normed = layer_norm(stream, norm_gain)
    features = jnp.dot(
        normed, proj_weight, precision=highest, preferred_element_type=f32
    ).astype(bf16)
    channels = features.shape[1]
    features = features.reshape(local_frames, strip_tokens, channels)
    forward = [(i, i + 1) for i in range(head_groups - 1)]
    backward = [(i + 1, i) for i in range(head_groups - 1)]
    above = lax.ppermute(features[:, strip_tokens - GRID :], "head", forward)
    below = lax.ppermute(features[:, :GRID], "head", backward)
    extended = jnp.concatenate([above, features, below], axis=1)
    place = jnp.stack(
        [lax.axis_index("head").astype(jnp.int32), jnp.full((), head_groups, jnp.int32)]
    )
    return predict(extended, up_weight, conv_weight, conv_bias, place, strip_tokens // GRID)


def solution(mesh):
    in_specs = (
        P("frame", "head", None),
        P(),
        P(),
        P(),
        P(),
        P(),
        P(),
        P(),
        P("frame", None),
        P("frame"),
    )
    out_specs = P("frame", "head", None, None)
    return jax.shard_map(
        on_device, mesh=mesh, in_specs=in_specs, out_specs=out_specs, check_vma=False
    )
```
